512 devices in a mesh: row: 16 (over y_hi, x, core), col: 32 (over z, y_lo).
Axes of the slice: x: 4, y: 4 (y_hi: 2, y_lo: 2; y = y_hi * 2 + y_lo), z: 16, core: 2. Of those that a mesh axis runs over, the one named last changes fastest.
Arguments:
- history: bfloat16 [16, 32, 32, 8, 128], P('row', 'col'), may hold values from -6 to 6
- tiles: bfloat16 [16, 32, 96, 128, 128], P('row', 'col'), may hold values from -0.078125 to 0.078125
- tile_target: int32 [16, 32, 96], P('row', 'col'), may hold values from 0 to 31
- tile_lag: int32 [16, 32, 96], P('row', 'col'), may hold values from 16 to 32
- tile_count: int32 [16, 32, 16], P('row', 'col'), may hold values from 0 to 6, as said below
- self_tiles: bfloat16 [16, 32, 32, 128, 128], P('row', 'col'), may hold values from -0.046875 to 0.046875
- near_inverse: float32 [16, 32, 128, 128], P('row', 'col'), may hold values from -0.5 to 0.5
- incident: float32 [16, 32, 16, 8, 128], P('row', 'col'), may hold values from -6 to 6
Outputs:
- density: float32 [16, 32, 16, 8, 128], P('row', 'col')
The draws below stay inside these ranges and needn't reach their ends.
Inputs may be any that keep to these rules, and one draw needn't show every extreme that they name: tile_count[g, c, h] is the number of live slots h * 6 .. h * 6 + 5 of device (g, c), which come first in that range; the other slots' entries are not read. Every device has 6 live slots for at least one row h.
All inputs are finite; a program needn't handle non-finite values.
Results may differ from the reference program's by a relative error of at most 0.0007.
Values may be sent and summed in bfloat16 or wider, within the bound.
No kernel may reach another device: no remote copies, remote signals or barrier semaphores. Data moves between devices by JAX's collectives and lax.ppermute only.
A program may use at most 64 MiB of HBM per device.

```python
import jax
import jax.numpy as jnp
from jax import lax

B = 128
E = 8
HIST = 32
K = 16
TPS = 6
GROUPS = 16
PANELS = 32
SLOTS = 96


def draw_tile_count(key, part):
    key_heavy, key_light, key_chosen = jax.random.split(jax.random.fold_in(key, 17), 3)
    heavy = jax.random.randint(key_heavy, (GROUPS, PANELS, 1), 0, 4) == 0
    light = jax.random.randint(key_light, (GROUPS, PANELS, GROUPS), 0, TPS // 2 + 1)
    base = jnp.where(heavy, TPS, light)
    chosen = jax.random.randint(key_chosen, (GROUPS, PANELS, 1), 0, GROUPS)
    group_range = jnp.arange(GROUPS, dtype=jnp.int32)[None, None, :]
    return jnp.where(group_range == chosen, TPS, base).astype(jnp.int32)


def place_ends(values, own_key, least, largest):
    shape = values.shape
    place = [jax.random.randint(jax.random.fold_in(own_key, axis), (), 0, shape[axis]) for axis in range(len(shape))]
    values = values.at[tuple(place)].set(least)
    longest = shape.index(max(shape))
    place[longest] = (place[longest] + 1) % shape[longest]
    return values.at[tuple(place)].set(largest)


def shard_levels(own_key, extent, cuts, smallest, largest):
    level, own = 1.0, jax.random.fold_in(own_key, 6)
    for position, parts in cuts:
        heights = jnp.exp(jax.random.uniform(jax.random.fold_in(own, position), (parts,), jnp.float32, smallest / len(cuts), largest / len(cuts)))
        level = level * jnp.repeat(heights, extent[position] // parts).reshape([-1 if axis == position else 1 for axis in range(len(extent))])
    return level


def centred(stream_key, shape, scale, reach, cuts=(), held_as=jnp.bfloat16):
    factor_of = shard_levels(stream_key, shape, cuts, -0.22, 0.18) if cuts else 1.0
    drawn = jax.random.normal(stream_key, shape, jnp.float32) * scale * factor_of
    return jnp.minimum(jnp.maximum(drawn, -reach), reach).astype(held_as)


def setup_inputs(seed: int = 0) -> dict:
    splits = jax.random.split(jax.random.key(seed), 9)
    return {
        "history": centred(splits[0], (GROUPS, PANELS, HIST, E, B), 1.0, 6.0, ((0, 16), (1, 32))),
        "tiles": centred(splits[1], (GROUPS, PANELS, SLOTS, B, B), (B * SLOTS // 2) ** -0.5, 0.078125, ((0, 16), (1, 32))),
        "tile_target": place_ends(jax.random.randint(splits[2], (GROUPS, PANELS, SLOTS), 0, PANELS), jax.random.fold_in(splits[2], 1), 0, PANELS - 1).astype(jnp.int32),
        "tile_lag": place_ends(jax.random.randint(splits[3], (GROUPS, PANELS, SLOTS), K, HIST + 1), jax.random.fold_in(splits[3], 1), K, HIST).astype(jnp.int32),
        "tile_count": draw_tile_count(jax.random.fold_in(splits[8], 71), 0),
        "self_tiles": centred(splits[5], (GROUPS, PANELS, HIST, B, B), (4 * B * HIST) ** -0.5, 0.046875, ((0, 16), (1, 32))),
        "near_inverse": centred(splits[6], (GROUPS, PANELS, B, B), B ** -0.5, 0.5, ((0, 16), (1, 32)), jnp.float32),
        "incident": centred(splits[7], (GROUPS, PANELS, K, E, B), 1.0, 6.0, ((0, 16), (1, 32)), jnp.float32),
    }


def reference(history, tiles, tile_target, tile_lag, tile_count, self_tiles, near_inverse, incident):
    step_range = jnp.arange(K, dtype=jnp.int32)
    panel_range = jnp.arange(PANELS, dtype=jnp.int32)
    slot_range = jnp.arange(SLOTS, dtype=jnp.int32)
    source_group = slot_range // TPS
    within_group = slot_range % TPS
    lag_range = jnp.arange(HIST, dtype=jnp.int32) + 1
    before = lag_range[:, None] > step_range[None, :]
    past_index = jnp.where(before, HIST + step_range[None, :] - lag_range[:, None], 0).astype(jnp.int32)

    def one_row(group_index):
        def one_device(partial_value, column_index):
            column_past = jnp.take(history, column_index, axis=1)
            flat_past = column_past.reshape(GROUPS * HIST, E, B)
            lags = tile_lag[group_index, column_index]
            counts = tile_count[group_index, column_index]
            live = within_group < counts[source_group]
            rows_index = (source_group[:, None] * HIST + HIST - lags[:, None] + step_range[None, :]).astype(jnp.int32)
            windows = flat_past[rows_index].astype(jnp.float32)
            products = jnp.einsum("skej,sji->skei", windows, tiles[group_index, column_index].astype(jnp.float32))
            selector = ((tile_target[group_index, column_index][None, :] == panel_range[:, None]) & live[None, :]).astype(jnp.float32)
            partial_value = partial_value + jnp.einsum("ts,skei->tkei", selector, products, precision=lax.Precision.HIGHEST)
            own_past = history[group_index, column_index]
            self_windows = own_past[past_index].astype(jnp.float32) * before[:, :, None, None].astype(jnp.float32)
            self_term = jnp.einsum("lkej,lji->kei", self_windows, self_tiles[group_index, column_index].astype(jnp.float32))
            return partial_value, self_term

        empty = jnp.zeros((PANELS, K, E, B), jnp.float32)
        return lax.scan(one_device, empty, panel_range)

    far, self_past = lax.map(one_row, jnp.arange(GROUPS, dtype=jnp.int32))
    fresh_list = []
    density_list = []
    for step_index in range(K):
        bracket = incident[:, :, step_index] - far[:, :, step_index] - self_past[:, :, step_index]
        for lag_index in range(1, step_index + 1):
            earlier = fresh_list[step_index - lag_index].astype(jnp.float32)
            lag_matrix = self_tiles[:, :, lag_index - 1].astype(jnp.float32)
            bracket = bracket - jnp.einsum("gcej,gcji->gcei", earlier, lag_matrix)
        density_now = jnp.einsum("gcej,gcji->gcei", bracket, near_inverse, precision=lax.Precision.HIGHEST)
        density_list.append(density_now)
        fresh_list.append(lax.optimization_barrier(density_now.astype(jnp.bfloat16)))
    return jnp.stack(density_list, axis=2)
```

```python
import functools

import jax
import jax.numpy as jnp
from jax import lax
from jax.experimental import pallas as pl
from jax.experimental.pallas import tpu as pltpu
from jax.sharding import Mesh, PartitionSpec as P

B = 128
E = 8
HIST = 32
K = 16
TPS = 6
GROUPS = 16
PANELS = 32
SLOTS = 96
ROWS = K * E
HALF = GROUPS // 2
CODE = 8
FULL = 32760.0

VMEM = pl.BlockSpec(memory_space=pltpu.VMEM)
SMEM = pl.BlockSpec(memory_space=pltpu.SMEM)
HIGHEST = lax.Precision.HIGHEST


def dot(a, b):
    return jnp.dot(a, b, preferred_element_type=jnp.float32)


def encode(values, store):
    peak = jnp.maximum(jnp.max(jnp.abs(values), axis=0, keepdims=True), 1e-30)
    code = jnp.floor(jnp.log2(peak)) + 1.0
    scaled = values * (jnp.exp2(-code) * FULL)
    store(0, ROWS, jnp.round(scaled).astype(jnp.int32).astype(jnp.int16))
    wide = jnp.broadcast_to(code, (CODE, B))
    store(ROWS, CODE, wide.astype(jnp.int32).astype(jnp.int16))


def decode(block):
    code = block[ROWS : ROWS + 1].astype(jnp.int32).astype(jnp.float32)
    scale = jnp.exp2(code) * (1.0 / FULL)
    return block[:ROWS].astype(jnp.int32).astype(jnp.float32) * scale


def add_products(side, lag, target, count, past, tiles, wide, total):
    wide[...] = past[...].astype(jnp.float32)

    def source(p, carry):
        h = 2 * p + side
        live = count[h]
        for j in range(TPS):
            s = h * TPS + j
            first = jnp.clip(HIST - lag[s], 0, HIST - K)
            place = jnp.where(j < live, jnp.clip(target[s], 0, PANELS - 1), PANELS)
            window = wide[p, pl.ds(first, K)].reshape(ROWS, B).astype(jnp.bfloat16)
            total[place] += dot(window, tiles[s])
        return carry

    lax.fori_loop(0, HALF, source, 0)


def near_kernel(core, lag, target, count, past, tiles, total, wide):
    total[...] = jnp.zeros_like(total)
    add_products(core[0], lag, target, count, past, tiles, wide, total)


def far_kernel(core, lag, target, count, past, tiles, before, out, wide, total):
    total[...] = before[...]
    add_products(1 - core[0], lag, target, count, past, tiles, wide, total)

    def pack(z, carry):
        for d in range(4):

            def store(at, n, v):
                out[d, z, pl.ds(at, n)] = v

            encode(total[z * 4 + d], store)
        return carry

    lax.fori_loop(0, PANELS // 4, pack, 0)


def merge_kernel(got, out):
    def merge(z, carry):
        value = decode(got[0, z])
        for d in range(1, 4):
            value = value + decode(got[d, z])

        def store(at, n, v):
            out[z, pl.ds(at, n)] = v

        encode(value, store)
        return carry

    lax.fori_loop(0, PANELS // 4, merge, 0)


def thirds(x):
    a = x.astype(jnp.bfloat16)
    rest = x - a.astype(jnp.float32)
    b = rest.astype(jnp.bfloat16)
    c = (rest - b.astype(jnp.float32)).astype(jnp.bfloat16)
    return a, b, c


def self_kernel(own, self_tiles, near, incident, base, steps, wide):
    wide[pl.ds(0, HIST)] = own[...].astype(jnp.float32)
    wide[pl.ds(HIST, K)] = jnp.zeros((K, E, B), jnp.float32)
    drive = incident[...].reshape(ROWS, B)
    for lag in range(1, HIST + 1):
        window = wide[pl.ds(HIST - lag, K)].reshape(ROWS, B).astype(jnp.bfloat16)
        drive = drive - dot(window, self_tiles[lag - 1])
    base[...] = jnp.dot(drive, near[...], precision=HIGHEST, preferred_element_type=jnp.float32)
    a, b, c = thirds(near[...])
    for lag in range(1, K):
        tile = self_tiles[lag - 1]
        m = dot(tile, a) + dot(tile, b) + dot(tile, c)
        high = m.astype(jnp.bfloat16)
        steps[lag - 1, pl.ds(0, B)] = high
        steps[lag - 1, pl.ds(B, B)] = (m - high.astype(jnp.float32)).astype(jnp.bfloat16)


def solve_kernel(got, near, base, steps, density):
    far = decode(got[0])
    for z in range(1, PANELS // 4):
        far = far + decode(got[z])
    drive = base[...] - jnp.dot(far, near[...], precision=HIGHEST, preferred_element_type=jnp.float32)
    rest = [drive[E * k : E * (k + 1)] for k in range(K)]
    for k in range(K):
        density[k] = rest[k]
        fresh = rest[k].astype(jnp.bfloat16)
        twice = jnp.concatenate([fresh, fresh], axis=1)
        for j in range(k + 1, K):
            rest[j] = rest[j] - dot(twice, steps[j - k - 1])


def call(kernel, outs, n_scalar, n_vector, scratch=(), **kw):
    single = not isinstance(outs, (tuple, list))
    return pl.pallas_call(
        kernel,
        out_shape=outs,
        in_specs=[SMEM] * n_scalar + [VMEM] * n_vector,
        out_specs=VMEM if single else [VMEM] * len(outs),
        scratch_shapes=list(scratch),
        compiler_params=pltpu.CompilerParams(vmem_limit_bytes=kw.get("limit", 24) << 20),
        cost_estimate=pl.CostEstimate(flops=kw.get("flops", 4 << 20), bytes_accessed=kw.get("bytes", 1 << 20), transcendentals=0),
        name=kw["name"],
    )


def local(history, tiles, tile_target, tile_lag, tile_count, self_tiles, near_inverse, incident):
    own = history[0, 0]
    core = lax.axis_index("core").astype(jnp.int32)[None]
    lag, target, count = tile_lag[0, 0], tile_target[0, 0], tile_count[0, 0]
    slot_tiles, near = tiles[0, 0], near_inverse[0, 0]
    wide = pltpu.VMEM((HALF, HIST, E, B), jnp.float32)
    total = jax.ShapeDtypeStruct((PANELS + 1, ROWS, B), jnp.float32)

    same = lax.all_to_all(jnp.broadcast_to(own, (HALF, HIST, E, B)), ("y_hi", "x"), 0, 0, tiled=True)
    other = lax.ppermute(same, "core", [(0, 1), (1, 0)])
    partial = call(near_kernel, total, 4, 2, [wide], name="near", flops=48 << 22, bytes=4 << 20)(
        core, lag, target, count, same, slot_tiles
    )
    base, steps = call(
        self_kernel,
        [jax.ShapeDtypeStruct((ROWS, B), jnp.float32), jax.ShapeDtypeStruct((K - 1, 2 * B, B), jnp.bfloat16)],
        0,
        4,
        [pltpu.VMEM((HIST + K, E, B), jnp.float32)],
        name="selfpast",
        flops=32 << 22,
        bytes=2 << 20,
    )(own, self_tiles[0, 0], near, incident[0, 0])
    blocks = call(
        far_kernel,
        jax.ShapeDtypeStruct((4, PANELS // 4, ROWS + CODE, B), jnp.int16),
        4,
        3,
        [wide, pltpu.VMEM((PANELS + 1, ROWS, B), jnp.float32)],
        name="far",
        flops=48 << 22,
        bytes=6 << 20,
    )(core, lag, target, count, other, slot_tiles, partial)
    got = lax.all_to_all(blocks, ("z_lo", "y_lo"), 0, 0, tiled=True)
    merged = call(
        merge_kernel, jax.ShapeDtypeStruct((PANELS // 4, ROWS + CODE, B), jnp.int16), 0, 1, name="merge"
    )(got)
    got = lax.all_to_all(merged, "z_hi", 0, 0, tiled=True)
    density = call(solve_kernel, jax.ShapeDtypeStruct((K, E, B), jnp.float32), 0, 4, name="solve")(
        got, near, base, steps
    )
    return density[None, None]


def solution(mesh):
    fine = Mesh(mesh.devices.reshape(2, 4, 2, 8, 2, 2), ("y_hi", "x", "core", "z_hi", "z_lo", "y_lo"))
    row, col = ("y_hi", "x", "core"), ("z_hi", "z_lo", "y_lo")
    return jax.shard_map(
        local,
        mesh=fine,
        in_specs=(
            P(row, col, None, None, None),
            P(row, col, None, None, None),
            P(row, col, None),
            P(row, col, None),
            P(row, col, None),
            P(row, col, None, None, None),
            P(row, col, None, None),
            P(row, col, None, None, None),
        ),
        out_specs=P(row, col, None, None, None),
        check_vma=False,
    )
```

```python
import jax
import jax.numpy as jnp
from jax import lax
from jax.experimental import pallas as pl
from jax.experimental.pallas import tpu as pltpu
from jax.sharding import Mesh, PartitionSpec as P

B = 128
E = 8
HIST = 32
K = 16
TPS = 6
GROUPS = 16
PANELS = 32
SLOTS = 96
ROWS = K * E
HALF = GROUPS // 2
PART = 4
NEAR = 4
NEXT = PANELS // NEAR
FULL = 32760.0

VMEM = pl.BlockSpec(memory_space=pltpu.VMEM)
SMEM = pl.BlockSpec(memory_space=pltpu.SMEM)
HBM = pl.BlockSpec(memory_space=pltpu.HBM)
HIGHEST = lax.Precision.HIGHEST


def dot(a, b):
    return jnp.dot(a, b, preferred_element_type=jnp.float32)


def encode(values):
    peak = jnp.maximum(jnp.max(jnp.abs(values), axis=0, keepdims=True), 1e-30)
    code = jnp.floor(jnp.log2(peak)) + 1.0
    scaled = jnp.round(values * (jnp.exp2(-code) * FULL)).astype(jnp.int32)
    return scaled.reshape(K, E, B).astype(jnp.int16), code


def decode(values, scale):
    return values.astype(jnp.int32).astype(jnp.float32).reshape(ROWS, B) * scale


def scales(codes):
    return jnp.exp2(codes.astype(jnp.int32).astype(jnp.float32)) * (1.0 / FULL)


def add_products(side, lists, tables, past, tiles, wide, total, slab, tile_sem, list_sem, begin):
    loads = [pltpu.make_async_copy(a, b, list_sem.at[i]) for i, (a, b) in enumerate(zip(lists, tables))]
    for load in loads:
        load.start()

    def tile_load(p):
        return pltpu.make_async_copy(tiles.at[pl.ds((2 * p + side) * TPS, TPS)], slab.at[p], tile_sem.at[p])

    for p in range(HALF):
        tile_load(p).start()
    wide[...] = past[...].astype(jnp.float32)
    begin()
    for load in loads:
        load.wait()
    lag, target, count = tables

    def sources(part, carry):
        these = [part * PART + i for i in range(PART)]
        for p in these:
            tile_load(p).wait()
        for p in these:
            h = 2 * p + side
            live = count[h]
            for j in range(TPS):
                s = h * TPS + j
                first = jnp.clip(HIST - lag[s], 0, HIST - K)
                place = jnp.where(j < live, jnp.clip(target[s], 0, PANELS - 1), PANELS)
                window = wide[p, pl.ds(first, K)].reshape(ROWS, B).astype(jnp.bfloat16)
                total[place] += dot(window, slab[p, j])
        return carry

    lax.fori_loop(0, HALF // PART, sources, 0)


def near_kernel(core, lag, target, count, tiles, past, total, *scratch):
    def begin():
        total[...] = jnp.zeros_like(total)

    wide, slab, tile_sem, list_sem, *tables = scratch
    add_products(core[0], (lag, target, count), tables, past, tiles, wide, total, slab, tile_sem, list_sem, begin)


def far_kernel(core, lag, target, count, tiles, past, before, out, *scratch):
    wide, slab, tile_sem, list_sem, *tables, total = scratch

    def begin():
        total[...] = before[...]

    add_products(1 - core[0], (lag, target, count), tables, past, tiles, wide, total, slab, tile_sem, list_sem, begin)

    def pack(d, carry):
        codes = []
        for z in range(NEXT):
            values, code = encode(total[z * NEAR + d])
            out[d, pl.ds(z * K, K)] = values
            codes.append(code)
        out[d, NEXT * K] = jnp.concatenate(codes, axis=0).astype(jnp.int32).astype(jnp.int16)
        return carry

    lax.fori_loop(0, NEAR, pack, 0)


def merge_kernel(got, out):
    scale = [scales(got[d, NEXT * K]) for d in range(NEAR)]
    for z in range(NEXT):
        value = decode(got[0, pl.ds(z * K, K)], scale[0][z : z + 1])
        for d in range(1, NEAR):
            value = value + decode(got[d, pl.ds(z * K, K)], scale[d][z : z + 1])
        values, code = encode(value)
        out[z, pl.ds(0, K)] = values
        wide = jnp.broadcast_to(code, (E, B)).astype(jnp.int32).astype(jnp.int16)
        out[z, K] = wide


def thirds(x):
    a = x.astype(jnp.bfloat16)
    rest = x - a.astype(jnp.float32)
    b = rest.astype(jnp.bfloat16)
    c = (rest - b.astype(jnp.float32)).astype(jnp.bfloat16)
    return a, b, c


def self_kernel(own_h, self_h, near_h, incident_h, base, steps, wide, own, self_tiles, near, incident, sem):
    pairs = ((own_h, own), (self_h, self_tiles), (near_h, near), (incident_h, incident))
    loads = [pltpu.make_async_copy(a, b, sem.at[i]) for i, (a, b) in enumerate(pairs)]
    for load in loads:
        load.start()
    for load in loads:
        load.wait()
    wide[pl.ds(0, HIST)] = own[...].astype(jnp.float32)
    wide[pl.ds(HIST, K)] = jnp.zeros((K, E, B), jnp.float32)
    drive = incident[...].reshape(ROWS, B)
    for lag in range(1, HIST + 1):
        window = wide[pl.ds(HIST - lag, K)].reshape(ROWS, B).astype(jnp.bfloat16)
        drive = drive - dot(window, self_tiles[lag - 1])
    base[...] = jnp.dot(drive, near[...], precision=HIGHEST, preferred_element_type=jnp.float32)
    a, b, c = thirds(near[...])
    for lag in range(1, K):
        tile = self_tiles[lag - 1]
        m = dot(tile, a) + dot(tile, b) + dot(tile, c)
        high = m.astype(jnp.bfloat16)
        steps[lag - 1, pl.ds(0, B)] = high
        steps[lag - 1, pl.ds(B, B)] = (m - high.astype(jnp.float32)).astype(jnp.bfloat16)


def solve_kernel(got, near, base, steps, density):
    far = decode(got[0, pl.ds(0, K)], scales(got[0, K])[0:1])
    for z in range(1, NEXT):
        far = far + decode(got[z, pl.ds(0, K)], scales(got[z, K])[0:1])
    drive = base[...] - jnp.dot(far, near[...], precision=HIGHEST, preferred_element_type=jnp.float32)
    rest = [drive[E * k : E * (k + 1)] for k in range(K)]
    for k in range(K):
        density[k] = rest[k]
        fresh = rest[k].astype(jnp.bfloat16)
        twice = jnp.concatenate([fresh, fresh], axis=1)
        for j in range(k + 1, K):
            rest[j] = rest[j] - dot(twice, steps[j - k - 1])


def keep(x):
    return pltpu.with_memory_space_constraint(x, pltpu.HBM)


def call(kernel, outs, in_specs, scratch=(), **kw):
    single = not isinstance(outs, (tuple, list))
    return pl.pallas_call(
        kernel,
        out_shape=outs,
        in_specs=in_specs,
        out_specs=VMEM if single else [VMEM] * len(outs),
        scratch_shapes=list(scratch),
        compiler_params=pltpu.CompilerParams(vmem_limit_bytes=24 << 20),
        cost_estimate=pl.CostEstimate(flops=kw["flops"], bytes_accessed=kw["bytes"], transcendentals=0),
        name=kw["name"],
    )


def local(history, tiles, tile_target, tile_lag, tile_count, self_tiles, near_inverse, incident):
    own = history[0, 0]
    core = lax.axis_index("core").astype(jnp.int32)[None]
    lists = tuple(keep(x[0, 0]) for x in (tile_lag, tile_target, tile_count))
    slot_tiles, near = keep(tiles[0, 0]), keep(near_inverse[0, 0])
    total = (PANELS + 1, ROWS, B)
    scratch = [
        pltpu.VMEM((HALF, HIST, E, B), jnp.float32),
        pltpu.VMEM((HALF, TPS, B, B), jnp.bfloat16),
        pltpu.SemaphoreType.DMA((HALF,)),
        pltpu.SemaphoreType.DMA((3,)),
        pltpu.SMEM((SLOTS,), jnp.int32),
        pltpu.SMEM((SLOTS,), jnp.int32),
        pltpu.SMEM((GROUPS,), jnp.int32),
    ]

    same = lax.all_to_all(jnp.broadcast_to(own, (HALF, HIST, E, B)), ("y_hi", "x"), 0, 0, tiled=True)
    other = lax.ppermute(same, "core", [(0, 1), (1, 0)])
    partial = call(
        near_kernel,
        jax.ShapeDtypeStruct(total, jnp.float32),
        [SMEM, HBM, HBM, HBM, HBM, VMEM],
        scratch,
        name="near",
        flops=48 << 22,
        bytes=4 << 20,
    )(core, *lists, slot_tiles, same)
    blocks = call(
        far_kernel,
        jax.ShapeDtypeStruct((NEAR, NEXT * K + 1, E, B), jnp.int16),
        [SMEM, HBM, HBM, HBM, HBM, VMEM, VMEM],
        scratch + [pltpu.VMEM(total, jnp.float32)],
        name="far",
        flops=48 << 22,
        bytes=6 << 20,
    )(core, *lists, slot_tiles, other, partial)
    got = lax.all_to_all(blocks, ("z_lo", "y_lo"), 0, 0, tiled=True)
    merged = call(
        merge_kernel,
        jax.ShapeDtypeStruct((NEXT, K + 1, E, B), jnp.int16),
        [VMEM],
        name="merge",
        flops=1 << 20,
        bytes=2 << 20,
    )(got)
    got = lax.all_to_all(merged, "z_hi", 0, 0, tiled=True)
    base, steps = call(
        self_kernel,
        [jax.ShapeDtypeStruct((ROWS, B), jnp.float32), jax.ShapeDtypeStruct((K - 1, 2 * B, B), jnp.bfloat16)],
        [HBM, HBM, HBM, HBM],
        [
            pltpu.VMEM((HIST + K, E, B), jnp.float32),
            pltpu.VMEM((HIST, E, B), jnp.bfloat16),
            pltpu.VMEM((HIST, B, B), jnp.bfloat16),
            pltpu.VMEM((B, B), jnp.float32),
            pltpu.VMEM((K, E, B), jnp.float32),
            pltpu.SemaphoreType.DMA((4,)),
        ],
        name="selfpast",
        flops=32 << 22,
        bytes=2 << 20,
    )(keep(own), keep(self_tiles[0, 0]), near, keep(incident[0, 0]))
    density = call(
        solve_kernel,
        jax.ShapeDtypeStruct((K, E, B), jnp.float32),
        [VMEM] * 4,
        name="solve",
        flops=16 << 22,
        bytes=2 << 20,
    )(got, near_inverse[0, 0], base, steps)
    return density[None, None]


def solution(mesh):
    fine = Mesh(mesh.devices.reshape(2, 4, 2, 8, 2, 2), ("y_hi", "x", "core", "z_hi", "z_lo", "y_lo"))
    row, col = ("y_hi", "x", "core"), ("z_hi", "z_lo", "y_lo")
    return jax.shard_map(
        local,
        mesh=fine,
        in_specs=(
            P(row, col, None, None, None),
            P(row, col, None, None, None),
            P(row, col, None),
            P(row, col, None),
            P(row, col, None),
            P(row, col, None, None, None),
            P(row, col, None, None),
            P(row, col, None, None, None),
        ),
        out_specs=P(row, col, None, None, None),
        check_vma=False,
    )
```

```python
import jax
import jax.numpy as jnp
from jax import lax
from jax.experimental import pallas as pl
from jax.experimental.pallas import tpu as pltpu
from jax.sharding import Mesh, PartitionSpec as P

B = 128
E = 8
HIST = 32
K = 16
TPS = 6
GROUPS = 16
PANELS = 32
SLOTS = 96
ROWS = K * E
HALF = GROUPS // 2
PART = 4
NEAR = 4
NEXT = PANELS // NEAR
FULL = 32760.0
NEAR_GROUPS = [[NEAR * s + d for d in range(NEAR)] for s in range(NEXT)]
NEXT_GROUPS = [[NEAR * s + (d ^ (2 * (s >= NEXT // 2))) for s in range(NEXT)] for d in range(NEAR)]

VMEM = pl.BlockSpec(memory_space=pltpu.VMEM)
SMEM = pl.BlockSpec(memory_space=pltpu.SMEM)
HBM = pl.BlockSpec(memory_space=pltpu.HBM)
HIGHEST = lax.Precision.HIGHEST


def dot(a, b):
    return jnp.dot(a, b, preferred_element_type=jnp.float32)


def encode(values):
    peak = jnp.maximum(jnp.max(jnp.abs(values), axis=0, keepdims=True), 1e-30)
    code = jnp.floor(jnp.log2(peak)) + 1.0
    scaled = jnp.round(values * (jnp.exp2(-code) * FULL)).astype(jnp.int32)
    return scaled.reshape(K, E, B).astype(jnp.int16), code


def decode(values, scale):
    return values.astype(jnp.int32).astype(jnp.float32).reshape(ROWS, B) * scale


def scales(codes):
    return jnp.exp2(codes.astype(jnp.int32).astype(jnp.float32)) * (1.0 / FULL)


def add_products(side, lists, tables, past, tiles, wide, total, slab, tile_sem, list_sem, begin):
    loads = [pltpu.make_async_copy(a, b, list_sem.at[i]) for i, (a, b) in enumerate(zip(lists, tables))]
    for load in loads:
        load.start()

    def tile_load(p):
        return pltpu.make_async_copy(tiles.at[pl.ds((2 * p + side) * TPS, TPS)], slab.at[p], tile_sem.at[p])

    for p in range(HALF):
        tile_load(p).start()
    wide[...] = past[...].astype(jnp.float32)
    begin()
    for load in loads:
        load.wait()
    lag, target, count = tables

    def sources(part, carry):
        these = [part * PART + i for i in range(PART)]
        for p in these:
            tile_load(p).wait()
        for p in these:
            h = 2 * p + side
            live = count[h]
            for j in range(TPS):
                s = h * TPS + j
                first = jnp.clip(HIST - lag[s], 0, HIST - K)
                place = jnp.where(j < live, jnp.clip(target[s], 0, PANELS - 1), PANELS)
                window = wide[p, pl.ds(first, K)].reshape(ROWS, B).astype(jnp.bfloat16)
                total[place] += dot(window, slab[p, j])
        return carry

    lax.fori_loop(0, HALF // PART, sources, 0)


def near_kernel(core, lag, target, count, tiles, past, total, *scratch):
    def begin():
        total[...] = jnp.zeros_like(total)

    wide, slab, tile_sem, list_sem, *tables = scratch
    add_products(core[0], (lag, target, count), tables, past, tiles, wide, total, slab, tile_sem, list_sem, begin)


def far_kernel(core, far_half, lag, target, count, tiles, past, before, out, *scratch):
    wide, slab, tile_sem, list_sem, *tables, total = scratch

    def begin():
        total[...] = before[...]

    add_products(1 - core[0], (lag, target, count), tables, past, tiles, wide, total, slab, tile_sem, list_sem, begin)

    def pack(d, carry):
        codes = []
        for z in range(NEXT):
            swap = far_half[0] ^ (z >= NEXT // 2)
            values, code = encode(total[z * NEAR + (d ^ (2 * swap))])
            out[d, pl.ds(z * K, K)] = values
            codes.append(code)
        out[d, NEXT * K] = jnp.concatenate(codes, axis=0).astype(jnp.int32).astype(jnp.int16)
        return carry

    lax.fori_loop(0, NEAR, pack, 0)


def merge_kernel(got, out):
    scale = [scales(got[d, NEXT * K]) for d in range(NEAR)]
    for z in range(NEXT):
        value = decode(got[0, pl.ds(z * K, K)], scale[0][z : z + 1])
        for d in range(1, NEAR):
            value = value + decode(got[d, pl.ds(z * K, K)], scale[d][z : z + 1])
        values, code = encode(value)
        out[z, pl.ds(0, K)] = values
        wide = jnp.broadcast_to(code, (E, B)).astype(jnp.int32).astype(jnp.int16)
        out[z, K] = wide


def thirds(x):
    a = x.astype(jnp.bfloat16)
    rest = x - a.astype(jnp.float32)
    b = rest.astype(jnp.bfloat16)
    c = (rest - b.astype(jnp.float32)).astype(jnp.bfloat16)
    return a, b, c


def self_kernel(own_h, self_h, near_h, incident_h, base, steps, wide, own, self_tiles, near, incident, sem):
    pairs = ((own_h, own), (self_h, self_tiles), (near_h, near), (incident_h, incident))
    loads = [pltpu.make_async_copy(a, b, sem.at[i]) for i, (a, b) in enumerate(pairs)]
    for load in loads:
        load.start()
    for load in loads:
        load.wait()
    wide[pl.ds(0, HIST)] = own[...].astype(jnp.float32)
    wide[pl.ds(HIST, K)] = jnp.zeros((K, E, B), jnp.float32)
    drive = incident[...].reshape(ROWS, B)
    for lag in range(1, HIST + 1):
        window = wide[pl.ds(HIST - lag, K)].reshape(ROWS, B).astype(jnp.bfloat16)
        drive = drive - dot(window, self_tiles[lag - 1])
    base[...] = jnp.dot(drive, near[...], precision=HIGHEST, preferred_element_type=jnp.float32)
    a, b, c = thirds(near[...])
    for lag in range(1, K):
        tile = self_tiles[lag - 1]
        m = dot(tile, a) + dot(tile, b) + dot(tile, c)
        high = m.astype(jnp.bfloat16)
        steps[lag - 1, pl.ds(0, B)] = high
        steps[lag - 1, pl.ds(B, B)] = (m - high.astype(jnp.float32)).astype(jnp.bfloat16)


def solve_kernel(got, near, base, steps, density):
    far = decode(got[0, pl.ds(0, K)], scales(got[0, K])[0:1])
    for z in range(1, NEXT):
        far = far + decode(got[z, pl.ds(0, K)], scales(got[z, K])[0:1])
    drive = base[...] - jnp.dot(far, near[...], precision=HIGHEST, preferred_element_type=jnp.float32)
    rest = [drive[E * k : E * (k + 1)] for k in range(K)]
    for k in range(K):
        density[k] = rest[k]
        fresh = rest[k].astype(jnp.bfloat16)
        twice = jnp.concatenate([fresh, fresh], axis=1)
        for j in range(k + 1, K):
            rest[j] = rest[j] - dot(twice, steps[j - k - 1])


def keep(x):
    return pltpu.with_memory_space_constraint(x, pltpu.HBM)


def call(kernel, outs, in_specs, scratch=(), **kw):
    single = not isinstance(outs, (tuple, list))
    return pl.pallas_call(
        kernel,
        out_shape=outs,
        in_specs=in_specs,
        out_specs=VMEM if single else [VMEM] * len(outs),
        scratch_shapes=list(scratch),
        compiler_params=pltpu.CompilerParams(vmem_limit_bytes=24 << 20),
        cost_estimate=pl.CostEstimate(flops=kw["flops"], bytes_accessed=kw["bytes"], transcendentals=0),
        name=kw["name"],
    )


def local(history, tiles, tile_target, tile_lag, tile_count, self_tiles, near_inverse, incident):
    own = history[0, 0]
    core = lax.axis_index("core").astype(jnp.int32)[None]
    far_half = (lax.axis_index("col") >= PANELS // 2).astype(jnp.int32)[None]
    lists = tuple(keep(x[0, 0]) for x in (tile_lag, tile_target, tile_count))
    slot_tiles, near = keep(tiles[0, 0]), keep(near_inverse[0, 0])
    total = (PANELS + 1, ROWS, B)
    scratch = [
        pltpu.VMEM((HALF, HIST, E, B), jnp.float32),
        pltpu.VMEM((HALF, TPS, B, B), jnp.bfloat16),
        pltpu.SemaphoreType.DMA((HALF,)),
        pltpu.SemaphoreType.DMA((3,)),
        pltpu.SMEM((SLOTS,), jnp.int32),
        pltpu.SMEM((SLOTS,), jnp.int32),
        pltpu.SMEM((GROUPS,), jnp.int32),
    ]

    same = lax.all_to_all(jnp.broadcast_to(own, (HALF, HIST, E, B)), ("y_hi", "x"), 0, 0, tiled=True)
    other = lax.ppermute(same, "core", [(0, 1), (1, 0)])
    partial = call(
        near_kernel,
        jax.ShapeDtypeStruct(total, jnp.float32),
        [SMEM, HBM, HBM, HBM, HBM, VMEM],
        scratch,
        name="near",
        flops=48 << 22,
        bytes=4 << 20,
    )(core, *lists, slot_tiles, same)
    blocks = call(
        far_kernel,
        jax.ShapeDtypeStruct((NEAR, NEXT * K + 1, E, B), jnp.int16),
        [SMEM, SMEM, HBM, HBM, HBM, HBM, VMEM, VMEM],
        scratch + [pltpu.VMEM(total, jnp.float32)],
        name="far",
        flops=48 << 22,
        bytes=6 << 20,
    )(core, far_half, *lists, slot_tiles, other, partial)
    got = lax.all_to_all(blocks, "col", 0, 0, tiled=True, axis_index_groups=NEAR_GROUPS)
    merged = call(
        merge_kernel,
        jax.ShapeDtypeStruct((NEXT, K + 1, E, B), jnp.int16),
        [VMEM],
        name="merge",
        flops=1 << 20,
        bytes=2 << 20,
    )(got)
    got = lax.all_to_all(merged, "col", 0, 0, tiled=True, axis_index_groups=NEXT_GROUPS)
    base, steps = call(
        self_kernel,
        [jax.ShapeDtypeStruct((ROWS, B), jnp.float32), jax.ShapeDtypeStruct((K - 1, 2 * B, B), jnp.bfloat16)],
        [HBM, HBM, HBM, HBM],
        [
            pltpu.VMEM((HIST + K, E, B), jnp.float32),
            pltpu.VMEM((HIST, E, B), jnp.bfloat16),
            pltpu.VMEM((HIST, B, B), jnp.bfloat16),
            pltpu.VMEM((B, B), jnp.float32),
            pltpu.VMEM((K, E, B), jnp.float32),
            pltpu.SemaphoreType.DMA((4,)),
        ],
        name="selfpast",
        flops=32 << 22,
        bytes=2 << 20,
    )(keep(own), keep(self_tiles[0, 0]), near, keep(incident[0, 0]))
    density = call(
        solve_kernel,
        jax.ShapeDtypeStruct((K, E, B), jnp.float32),
        [VMEM] * 4,
        name="solve",
        flops=16 << 22,
        bytes=2 << 20,
    )(got, near_inverse[0, 0], base, steps)
    return density[None, None]


def solution(mesh):
    fine = Mesh(mesh.devices.reshape(2, 4, 2, PANELS), ("y_hi", "x", "core", "col"))
    row, col = ("y_hi", "x", "core"), "col"
    return jax.shard_map(
        local,
        mesh=fine,
        in_specs=(
            P(row, col, None, None, None),
            P(row, col, None, None, None),
            P(row, col, None),
            P(row, col, None),
            P(row, col, None),
            P(row, col, None, None, None),
            P(row, col, None, None),
            P(row, col, None, None, None),
        ),
        out_specs=P(row, col, None, None, None),
        check_vma=False,
    )
```

```python
import jax
import jax.numpy as jnp
from jax import lax
from jax.experimental import pallas as pl
from jax.experimental.pallas import tpu as pltpu
from jax.sharding import Mesh, PartitionSpec as P

B = 128
E = 8
HIST = 32
K = 16
TPS = 6
GROUPS = 16
PANELS = 32
SLOTS = 96
ROWS = K * E
HALF = GROUPS // 2
PART = 4
NEAR = 4
NEXT = PANELS // NEAR
UNITS = K // 2
FULL = 32760.0
NEAR_GROUPS = [
    [PANELS * c + (NEAR * s + d + 2 * c) % PANELS for d in range(NEAR)] for c in range(2) for s in range(NEXT)
]
NEXT_GROUPS = [
    [PANELS * c + (NEAR * s + (d ^ (2 * (s >= NEXT // 2))) + 2 * c) % PANELS for s in range(NEXT)]
    for c in range(2)
    for d in range(NEAR)
]

VMEM = pl.BlockSpec(memory_space=pltpu.VMEM)
SMEM = pl.BlockSpec(memory_space=pltpu.SMEM)
HBM = pl.BlockSpec(memory_space=pltpu.HBM)
HIGHEST = lax.Precision.HIGHEST


def dot(a, b):
    return jnp.dot(a, b, preferred_element_type=jnp.float32)


def encode(values):
    peak = jnp.maximum(jnp.max(jnp.abs(values), axis=0, keepdims=True), 1e-30)
    code = jnp.floor(jnp.log2(peak)) + 1.0
    scaled = jnp.round(values * (jnp.exp2(-code) * FULL)).astype(jnp.int32)
    return scaled, code


def decode(values, scale):
    return values.astype(jnp.int32).astype(jnp.float32).reshape(ROWS, B) * scale


def scales(codes):
    return jnp.exp2(codes.astype(jnp.int32).astype(jnp.float32)) * (1.0 / FULL)


def add_products(side, lists, tables, past, tiles, wide, total, slab, tile_sem, list_sem, begin):
    loads = [pltpu.make_async_copy(a, b, list_sem.at[i]) for i, (a, b) in enumerate(zip(lists, tables))]
    for load in loads:
        load.start()

    def tile_load(p):
        return pltpu.make_async_copy(tiles.at[pl.ds((2 * p + side) * TPS, TPS)], slab.at[p], tile_sem.at[p])

    for p in range(HALF):
        tile_load(p).start()
    wide[...] = past[...].astype(jnp.float32)
    begin()
    for load in loads:
        load.wait()
    lag, target, count = tables

    def sources(part, carry):
        these = [part * PART + i for i in range(PART)]
        for p in these:
            tile_load(p).wait()
        for p in these:
            h = 2 * p + side
            live = count[h]
            for j in range(TPS):
                s = h * TPS + j
                first = jnp.clip(HIST - lag[s], 0, HIST - K)
                place = jnp.where(j < live, jnp.clip(target[s], 0, PANELS - 1), PANELS)
                window = wide[p, pl.ds(first, K)].reshape(ROWS, B).astype(jnp.bfloat16)
                total[place] += dot(window, slab[p, j])
        return carry

    lax.fori_loop(0, HALF // PART, sources, 0)


def near_kernel(core, lag, target, count, tiles, past, total, *scratch):
    def begin():
        total[...] = jnp.zeros_like(total)

    wide, slab, tile_sem, list_sem, *tables = scratch
    add_products(core[0], (lag, target, count), tables, past, tiles, wide, total, slab, tile_sem, list_sem, begin)


def far_kernel(core, far_half, lag, target, count, tiles, past, before, out, *scratch):
    wide, slab, tile_sem, list_sem, *tables, total = scratch

    def begin():
        total[...] = before[...]

    add_products(1 - core[0], (lag, target, count), tables, past, tiles, wide, total, slab, tile_sem, list_sem, begin)

    def pack(d, carry):
        codes = []
        for z in range(NEXT):
            swap = far_half[0] ^ (z >= NEXT // 2)
            place = z * NEAR + (d ^ (2 * swap)) + 2 * core[0]
            values, code = encode(total[lax.rem(place, PANELS)])
            out[d, pl.ds(z * UNITS, UNITS)] = values.reshape(UNITS, 2 * E, B).astype(jnp.int16)
            codes.append(code)
        rows = jnp.concatenate(codes + codes, axis=0)
        out[d, NEXT * UNITS] = rows.astype(jnp.int32).astype(jnp.int16)
        return carry

    lax.fori_loop(0, NEAR, pack, 0)


def merge_kernel(got, out):
    scale = [scales(got[d, NEXT * UNITS]) for d in range(NEAR)]
    for z in range(NEXT):
        value = decode(got[0, pl.ds(z * UNITS, UNITS)], scale[0][z : z + 1])
        for d in range(1, NEAR):
            value = value + decode(got[d, pl.ds(z * UNITS, UNITS)], scale[d][z : z + 1])
        values, code = encode(value)
        out[z, pl.ds(0, K)] = values.reshape(K, E, B).astype(jnp.int16)
        wide = jnp.broadcast_to(code, (E, B)).astype(jnp.int32).astype(jnp.int16)
        out[z, K] = wide


def thirds(x):
    a = x.astype(jnp.bfloat16)
    rest = x - a.astype(jnp.float32)
    b = rest.astype(jnp.bfloat16)
    c = (rest - b.astype(jnp.float32)).astype(jnp.bfloat16)
    return a, b, c


def self_kernel(own_h, self_h, near_h, incident_h, base, steps, wide, own, self_tiles, near, incident, sem):
    pairs = ((own_h, own), (self_h, self_tiles), (near_h, near), (incident_h, incident))
    loads = [pltpu.make_async_copy(a, b, sem.at[i]) for i, (a, b) in enumerate(pairs)]
    for load in loads:
        load.start()
    for load in loads:
        load.wait()
    wide[pl.ds(0, HIST)] = own[...].astype(jnp.float32)
    wide[pl.ds(HIST, K)] = jnp.zeros((K, E, B), jnp.float32)
    drive = incident[...].reshape(ROWS, B)
    for lag in range(1, HIST + 1):
        window = wide[pl.ds(HIST - lag, K)].reshape(ROWS, B).astype(jnp.bfloat16)
        drive = drive - dot(window, self_tiles[lag - 1])
    base[...] = jnp.dot(drive, near[...], precision=HIGHEST, preferred_element_type=jnp.float32)
    a, b, c = thirds(near[...])
    for lag in range(1, K):
        tile = self_tiles[lag - 1]
        m = dot(tile, a) + dot(tile, b) + dot(tile, c)
        high = m.astype(jnp.bfloat16)
        steps[lag - 1, pl.ds(0, B)] = high
        steps[lag - 1, pl.ds(B, B)] = (m - high.astype(jnp.float32)).astype(jnp.bfloat16)


def solve_kernel(got, near, base, steps, density):
    far = decode(got[0, pl.ds(0, K)], scales(got[0, K])[0:1])
    for z in range(1, NEXT):
        far = far + decode(got[z, pl.ds(0, K)], scales(got[z, K])[0:1])
    drive = base[...] - jnp.dot(far, near[...], precision=HIGHEST, preferred_element_type=jnp.float32)
    rest = [drive[E * k : E * (k + 1)] for k in range(K)]
    for k in range(K):
        density[k] = rest[k]
        fresh = rest[k].astype(jnp.bfloat16)
        twice = jnp.concatenate([fresh, fresh], axis=1)
        for j in range(k + 1, K):
            rest[j] = rest[j] - dot(twice, steps[j - k - 1])


def keep(x):
    return pltpu.with_memory_space_constraint(x, pltpu.HBM)


def call(kernel, outs, in_specs, scratch=(), **kw):
    single = not isinstance(outs, (tuple, list))
    return pl.pallas_call(
        kernel,
        out_shape=outs,
        in_specs=in_specs,
        out_specs=VMEM if single else [VMEM] * len(outs),
        scratch_shapes=list(scratch),
        compiler_params=pltpu.CompilerParams(vmem_limit_bytes=24 << 20),
        cost_estimate=pl.CostEstimate(flops=kw["flops"], bytes_accessed=kw["bytes"], transcendentals=0),
        name=kw["name"],
    )


def local(history, tiles, tile_target, tile_lag, tile_count, self_tiles, near_inverse, incident):
    own = history[0, 0]
    side = lax.axis_index("core").astype(jnp.int32)
    core = side[None]
    place = (lax.axis_index("col").astype(jnp.int32) + PANELS - 2 * side) % PANELS
    far_half = (place >= PANELS // 2).astype(jnp.int32)[None]
    lists = tuple(keep(x[0, 0]) for x in (tile_lag, tile_target, tile_count))
    slot_tiles, near = keep(tiles[0, 0]), keep(near_inverse[0, 0])
    total = (PANELS + 1, ROWS, B)
    scratch = [
        pltpu.VMEM((HALF, HIST, E, B), jnp.float32),
        pltpu.VMEM((HALF, TPS, B, B), jnp.bfloat16),
        pltpu.SemaphoreType.DMA((HALF,)),
        pltpu.SemaphoreType.DMA((3,)),
        pltpu.SMEM((SLOTS,), jnp.int32),
        pltpu.SMEM((SLOTS,), jnp.int32),
        pltpu.SMEM((GROUPS,), jnp.int32),
    ]

    same = lax.all_to_all(jnp.broadcast_to(own, (HALF, HIST, E, B)), ("y_hi", "x"), 0, 0, tiled=True)
    other = lax.ppermute(same, "core", [(0, 1), (1, 0)])
    partial = call(
        near_kernel,
        jax.ShapeDtypeStruct(total, jnp.float32),
        [SMEM, HBM, HBM, HBM, HBM, VMEM],
        scratch,
        name="near",
        flops=48 << 22,
        bytes=4 << 20,
    )(core, *lists, slot_tiles, same)
    blocks = call(
        far_kernel,
        jax.ShapeDtypeStruct((NEAR, NEXT * UNITS + 1, 2 * E, B), jnp.int16),
        [SMEM, SMEM, HBM, HBM, HBM, HBM, VMEM, VMEM],
        scratch + [pltpu.VMEM(total, jnp.float32)],
        name="far",
        flops=48 << 22,
        bytes=6 << 20,
    )(core, far_half, *lists, slot_tiles, other, partial)
    got = lax.all_to_all(blocks, ("core", "col"), 0, 0, tiled=True, axis_index_groups=NEAR_GROUPS)
    merged = call(
        merge_kernel,
        jax.ShapeDtypeStruct((NEXT, K + 1, E, B), jnp.int16),
        [VMEM],
        name="merge",
        flops=1 << 20,
        bytes=2 << 20,
    )(got)
    got = lax.all_to_all(merged, ("core", "col"), 0, 0, tiled=True, axis_index_groups=NEXT_GROUPS)
    base, steps = call(
        self_kernel,
        [jax.ShapeDtypeStruct((ROWS, B), jnp.float32), jax.ShapeDtypeStruct((K - 1, 2 * B, B), jnp.bfloat16)],
        [HBM, HBM, HBM, HBM],
        [
            pltpu.VMEM((HIST + K, E, B), jnp.float32),
            pltpu.VMEM((HIST, E, B), jnp.bfloat16),
            pltpu.VMEM((HIST, B, B), jnp.bfloat16),
            pltpu.VMEM((B, B), jnp.float32),
            pltpu.VMEM((K, E, B), jnp.float32),
            pltpu.SemaphoreType.DMA((4,)),
        ],
        name="selfpast",
        flops=32 << 22,
        bytes=2 << 20,
    )(keep(own), keep(self_tiles[0, 0]), near, keep(incident[0, 0]))
    density = call(
        solve_kernel,
        jax.ShapeDtypeStruct((K, E, B), jnp.float32),
        [VMEM] * 4,
        name="solve",
        flops=16 << 22,
        bytes=2 << 20,
    )(got, near_inverse[0, 0], base, steps)
    return density[None, None]


def solution(mesh):
    fine = Mesh(mesh.devices.reshape(2, 4, 2, PANELS), ("y_hi", "x", "core", "col"))
    row, col = ("y_hi", "x", "core"), "col"
    return jax.shard_map(
        local,
        mesh=fine,
        in_specs=(
            P(row, col, None, None, None),
            P(row, col, None, None, None),
            P(row, col, None),
            P(row, col, None),
            P(row, col, None),
            P(row, col, None, None, None),
            P(row, col, None, None),
            P(row, col, None, None, None),
        ),
        out_specs=P(row, col, None, None, None),
        check_vma=False,
    )
```
